32 devices in a mesh: ctx: 8 (over z, x), tp: 4 (over y, core).
Axes of the slice: x: 2, y: 2, z: 4, core: 2. Of those that a mesh axis runs over, the one named last changes fastest.
Arguments:
- inputs: bfloat16 [4096, 768], P(('ctx', 'tp')), may hold values from -6 to 6
- positions: int32 [4096], P('ctx'), may hold values from 0 to 3071, as said below
- attn_scale: float32 [768], replicated, may hold values from 0.1 to 1.9
- attn_shift: float32 [768], replicated, may hold values from -4 to 4
- mlp_scale: float32 [768], replicated, may hold values from 0.1 to 1.9
- mlp_shift: float32 [768], replicated, may hold values from -4 to 4
- qkv_weight: bfloat16 [768, 3, 768], P(None, None, 'tp'), may hold values from -0.21875 to 0.21875
- qv_bias: float32 [2, 768], P(None, 'tp'), may hold values from -4 to 4
- dense_weight: bfloat16 [768, 768], P('tp'), may hold values from -1.75 to 1.75
- dense_bias: float32 [768], replicated, may hold values from -5 to 5
- up_weight: bfloat16 [768, 3072], P(None, 'tp'), may hold values from -0.21875 to 0.21875
- up_bias: float32 [3072], P('tp'), may hold values from -4 to 4
- down_weight: bfloat16 [3072, 768], P('tp'), may hold values from -0.109375 to 0.109375
- down_bias: float32 [768], replicated, may hold values from -5 to 5
- cotangent: bfloat16 [4096, 768], P(('ctx', 'tp')), may hold values from -6 to 6
Outputs:
- output: bfloat16 [4096, 768], P(('ctx', 'tp'))
- grad_input: float32 [4096, 768], P(('ctx', 'tp'))
- grad_attn_scale: float32 [768], replicated
- grad_attn_shift: float32 [768], replicated
- grad_mlp_scale: float32 [768], replicated
- grad_mlp_shift: float32 [768], replicated
- grad_qkv: float32 [768, 3, 768], P(None, None, 'tp')
- grad_qv_bias: float32 [2, 768], P(None, 'tp')
- grad_dense: float32 [768, 768], P('tp')
- grad_dense_bias: float32 [768], replicated
- grad_up: float32 [768, 3072], P(None, 'tp')
- grad_up_bias: float32 [3072], P('tp')
- grad_down: float32 [3072, 768], P('tp')
- grad_down_bias: float32 [768], replicated
The draws below stay inside these ranges and needn't reach their ends.
Inputs may be any that keep to these rules, and one draw needn't show every extreme that they name: The sequence holds three documents; positions count from 0 at each document's first token and rise by one along it; the second document has 3072 tokens and starts at a token between 1 and 1023.
All inputs are finite; a program needn't handle non-finite values.
Results may differ from the reference program's by a relative error of at most 0.025.
Values may be sent and summed in bfloat16 or wider, within the bound.
A program may use at most 128 MiB of HBM per device.

```python
import jax
import jax.numpy as jnp
from jax import lax

D = 768
H = 12
HD = 64
ROT = 16
FF = 3072
TOKENS = 4096


def draw_positions(key, part):
    start_draw = jax.random.fold_in(key, 17)
    long_start = jax.random.randint(start_draw, (), 1, TOKENS // 4)
    long_end = long_start + 3 * TOKENS // 4
    places = jnp.arange(TOKENS, dtype=jnp.int32)
    doc_start = jnp.where(places >= long_end, long_end, jnp.where(places >= long_start, long_start, 0))
    return (places - doc_start).astype(jnp.int32)


def shard_levels(own_key, shape, shards, low, largest):
    loudness = 1.0
    for position, shards_of in shards:
        steps = jax.random.uniform(jax.random.fold_in(jax.random.fold_in(own_key, 6), position), (shards_of,), jnp.float32, low / len(shards), largest / len(shards))
        loudness = loudness * jnp.repeat(jnp.exp(steps), shape[position] // shards_of).reshape((-1,) + (1,) * (len(shape) - 1 - position))
    return loudness


def scatter_about(own_key, shape, spread, bound, split=(), held_as=jnp.bfloat16):
    drawn = spread * jax.random.normal(own_key, shape, jnp.float32)
    if split:
        drawn = drawn * shard_levels(own_key, shape, split, -0.22, 0.18)
    return jnp.clip(drawn, -bound, bound).astype(held_as)


def setup_inputs(seed: int = 0) -> dict:
    arg_keys = jax.random.split(jax.random.key(seed), 16)
    inputs = scatter_about(arg_keys[0], (TOKENS, D), 1.0, 6.0, ((0, 32),))
    positions = draw_positions(jax.random.fold_in(arg_keys[15], 71), 0)
    attn_scale = jnp.clip(1.0 + 0.18 * jax.random.normal(arg_keys[2], (D,), jnp.float32), 0.1, 1.9)
    attn_shift = scatter_about(arg_keys[3], (D,), 1.0, 4.0, (), jnp.float32)
    mlp_scale = jnp.clip(1.0 + 0.18 * jax.random.normal(arg_keys[4], (D,), jnp.float32), 0.1, 1.9)
    mlp_shift = scatter_about(arg_keys[5], (D,), 1.0, 4.0, (), jnp.float32)
    qkv_weight = scatter_about(arg_keys[6], (D, 3, H * HD), D ** -0.5, 0.21875, ((2, 4),))
    qv_bias = scatter_about(arg_keys[7], (2, H * HD), 1.0, 4.0, ((1, 4),), jnp.float32)
    dense_weight = scatter_about(arg_keys[8], (H * HD, D), (H * HD // 64) ** -0.5, 1.75, ((0, 4),))
    dense_bias = scatter_about(arg_keys[9], (D,), 1.25, 5.0, (), jnp.float32)
    up_weight = scatter_about(arg_keys[10], (D, FF), D ** -0.5, 0.21875, ((1, 4),))
    up_bias = scatter_about(arg_keys[11], (FF,), 1.0, 4.0, ((0, 4),), jnp.float32)
    down_weight = scatter_about(arg_keys[12], (FF, D), FF ** -0.5, 0.109375, ((0, 4),))
    down_bias = scatter_about(arg_keys[13], (D,), 1.25, 5.0, (), jnp.float32)
    cotangent = scatter_about(arg_keys[14], (TOKENS, D), 1.0, 6.0, ((0, 32),))
    return {"inputs": inputs, "positions": positions, "attn_scale": attn_scale, "attn_shift": attn_shift, "mlp_scale": mlp_scale, "mlp_shift": mlp_shift, "qkv_weight": qkv_weight, "qv_bias": qv_bias, "dense_weight": dense_weight, "dense_bias": dense_bias, "up_weight": up_weight, "up_bias": up_bias, "down_weight": down_weight, "down_bias": down_bias, "cotangent": cotangent}


norm_eps = 1e-05

def layer_norm(values, scale, shift):
    mean_value = lax.optimization_barrier(jnp.mean(values, axis=-1, keepdims=True))
    centred = values - mean_value
    variance = lax.optimization_barrier(jnp.mean(centred * centred, axis=-1, keepdims=True))
    inv_std = lax.rsqrt(variance + norm_eps)
    normal_part = centred * inv_std
    return (normal_part * scale + shift, normal_part, inv_std)

def norm_backward(grad_normed, normal_part, inv_std, scale):
    grad_hat = grad_normed * scale
    mean_grad = lax.optimization_barrier(jnp.mean(grad_hat, axis=-1, keepdims=True))
    mean_mixed = lax.optimization_barrier(jnp.mean(grad_hat * normal_part, axis=-1, keepdims=True))
    return inv_std * (grad_hat - mean_grad - normal_part * mean_mixed)

def rotary_tables(positions):
    freqs = 10000.0 ** (-jnp.arange(0, ROT, 2).astype(jnp.float32) / ROT)
    angles = positions.astype(jnp.float32)[:, None] * freqs[None, :]
    angles = jnp.concatenate([angles, angles], axis=1)
    return (jnp.cos(angles), jnp.sin(angles))

def rotate(tensor, cosines, sines):
    part = tensor[..., :ROT]
    half = ROT // 2
    turned = jnp.concatenate([-part[..., half:], part[..., :half]], axis=-1)
    spun = part * cosines[:, None, :] + turned * sines[:, None, :]
    return jnp.concatenate([spun, tensor[..., ROT:]], axis=-1)

def gelu_grad(pre_act):
    cumulative = 0.5 * (1.0 + jax.scipy.special.erf(pre_act * 0.7071067811865476))
    density = jnp.exp(-0.5 * pre_act * pre_act) * 0.3989422804014327
    return cumulative + pre_act * density

def reference(inputs, positions, attn_scale, attn_shift, mlp_scale, mlp_shift, qkv_weight, qv_bias, dense_weight, dense_bias, up_weight, up_bias, down_weight, down_bias, cotangent):
    width = H * HD
    score_scale = HD ** (-0.5)
    resid = inputs.astype(jnp.float32)
    normed_one, hat_one, std_one = layer_norm(resid, attn_scale, attn_shift)
    normed_two, hat_two, std_two = layer_norm(resid, mlp_scale, mlp_shift)
    attn_in = normed_one.astype(jnp.bfloat16)
    mlp_in = normed_two.astype(jnp.bfloat16)
    proj = jnp.dot(attn_in, qkv_weight.reshape(D, 3 * width), preferred_element_type=jnp.float32)
    proj = proj.reshape(TOKENS, 3, H, HD)
    cosines, sines = rotary_tables(positions)
    queries = rotate(proj[:, 0] + qv_bias[0].reshape(H, HD), cosines, sines).astype(jnp.bfloat16)
    keys_rot = rotate(proj[:, 1], cosines, sines).astype(jnp.bfloat16)
    values = (proj[:, 2] + qv_bias[1].reshape(H, HD)).astype(jnp.bfloat16)
    places = jnp.arange(TOKENS, dtype=jnp.int32)
    first_key = (places - positions).astype(jnp.int32)
    block = min(256, TOKENS)
    count = TOKENS // block
    key_float = keys_rot.astype(jnp.float32)
    value_float = values.astype(jnp.float32)

    def block_scores(number):
        start_row = (number * block).astype(jnp.int32)
        query_block = lax.dynamic_slice_in_dim(queries, start_row, block, 0).astype(jnp.float32)
        query_pos = start_row + jnp.arange(block, dtype=jnp.int32)
        first_block = lax.dynamic_slice_in_dim(first_key, start_row, block, 0)
        visible = (places[None, :] <= query_pos[:, None]) & (places[None, :] >= first_block[:, None])
        scores = jnp.einsum('qhd,khd->hqk', query_block, key_float) * score_scale
        return (start_row, query_block, visible, scores)

    def forward_block(number):
        start_row, query_block, visible, scores = block_scores(number)
        scores = jnp.where(visible[None], scores, -1e+30)
        row_max = lax.optimization_barrier(jnp.max(scores, axis=-1))
        weights = jnp.where(visible[None], jnp.exp(scores - row_max[..., None]), 0.0)
        row_sum = lax.optimization_barrier(jnp.sum(weights, axis=-1))
        low = lax.optimization_barrier(weights.astype(jnp.bfloat16)).astype(jnp.float32)
        summed = jnp.einsum('hqk,khd->qhd', low, value_float)
        attended = summed / jnp.transpose(row_sum)[:, :, None]
        return (attended.astype(jnp.bfloat16), row_max + jnp.log(row_sum))
    attended, log_total = lax.map(forward_block, jnp.arange(count))
    attended = attended.reshape(TOKENS, H, HD)
    attended_flat = attended.reshape(TOKENS, width)
    attn_part = jnp.dot(attended_flat, dense_weight, preferred_element_type=jnp.float32)
    pre_act = jnp.dot(mlp_in, up_weight, preferred_element_type=jnp.float32) + up_bias
    activation = jax.nn.gelu(pre_act, approximate=False).astype(jnp.bfloat16)
    mlp_part = jnp.dot(activation, down_weight, preferred_element_type=jnp.float32)
    output = (resid + (attn_part + mlp_part) + dense_bias + down_bias).astype(jnp.bfloat16)
    grad_out = cotangent.astype(jnp.float32)
    bias_grad = lax.optimization_barrier(jnp.sum(grad_out, axis=0))
    grad_down = jnp.dot(activation.T, cotangent, preferred_element_type=jnp.float32)
    grad_act = jnp.dot(cotangent, down_weight.T, preferred_element_type=jnp.float32)
    grad_pre = grad_act * gelu_grad(pre_act)
    grad_up_bias = lax.optimization_barrier(jnp.sum(grad_pre, axis=0))
    grad_pre_low = grad_pre.astype(jnp.bfloat16)
    grad_up = jnp.dot(mlp_in.T, grad_pre_low, preferred_element_type=jnp.float32)
    grad_mlp_in = jnp.dot(grad_pre_low, up_weight.T, preferred_element_type=jnp.float32)
    grad_dense = jnp.dot(attended_flat.T, cotangent, preferred_element_type=jnp.float32)
    grad_attended = jnp.dot(cotangent, dense_weight.T, preferred_element_type=jnp.float32)
    grad_attended = grad_attended.astype(jnp.bfloat16).reshape(TOKENS, H, HD)
    grad_att_float = grad_attended.astype(jnp.float32)
    delta_rows = lax.optimization_barrier(jnp.sum(grad_att_float * attended.astype(jnp.float32), axis=-1))

    def backward_step(carried, number):
        key_grad, value_grad = carried
        start_row, query_block, visible, scores = block_scores(number)
        grad_block = lax.dynamic_slice_in_dim(grad_att_float, start_row, block, 0)
        delta_block = lax.dynamic_slice_in_dim(delta_rows, start_row, block, 0)
        weights = jnp.where(visible[None], jnp.exp(scores - log_total[number][..., None]), 0.0)
        low = lax.optimization_barrier(weights.astype(jnp.bfloat16)).astype(jnp.float32)
        grad_weights = jnp.einsum('qhd,khd->hqk', grad_block, value_float)
        grad_scores = weights * (grad_weights - jnp.transpose(delta_block)[..., None])
        grad_low = lax.optimization_barrier(grad_scores.astype(jnp.bfloat16)).astype(jnp.float32)
        query_grad = jnp.einsum('hqk,khd->qhd', grad_low, key_float) * score_scale
        key_grad = key_grad + jnp.einsum('hqk,qhd->khd', grad_low, query_block) * score_scale
        value_grad = value_grad + jnp.einsum('hqk,qhd->khd', low, grad_block)
        return ((key_grad, value_grad), query_grad)
    zero_grads = (jnp.zeros((TOKENS, H, HD), jnp.float32), jnp.zeros((TOKENS, H, HD), jnp.float32))
    (key_grad, value_grad), query_grad = lax.scan(backward_step, zero_grads, jnp.arange(count))
    query_grad = query_grad.reshape(TOKENS, H, HD)
    grad_query_pre = rotate(query_grad, cosines, -sines)
    grad_key_pre = rotate(key_grad, cosines, -sines)
    grad_qv_bias = jnp.stack([lax.optimization_barrier(jnp.sum(grad_query_pre, axis=0)).reshape(width), lax.optimization_barrier(jnp.sum(value_grad, axis=0)).reshape(width)])
    grad_proj = jnp.stack([grad_query_pre, grad_key_pre, value_grad], axis=1)
    grad_proj = grad_proj.reshape(TOKENS, 3 * width).astype(jnp.bfloat16)
    grad_qkv = jnp.dot(attn_in.T, grad_proj, preferred_element_type=jnp.float32).reshape(D, 3, width)
    grad_attn_in = jnp.dot(grad_proj, qkv_weight.reshape(D, 3 * width).T, preferred_element_type=jnp.float32)
    grad_input = grad_out + norm_backward(grad_attn_in, hat_one, std_one, attn_scale)
    grad_input = grad_input + norm_backward(grad_mlp_in, hat_two, std_two, mlp_scale)
    grad_attn_scale = lax.optimization_barrier(jnp.sum(grad_attn_in * hat_one, axis=0))
    grad_attn_shift = lax.optimization_barrier(jnp.sum(grad_attn_in, axis=0))
    grad_mlp_scale = lax.optimization_barrier(jnp.sum(grad_mlp_in * hat_two, axis=0))
    grad_mlp_shift = lax.optimization_barrier(jnp.sum(grad_mlp_in, axis=0))
    return (output, grad_input, grad_attn_scale, grad_attn_shift, grad_mlp_scale, grad_mlp_shift, grad_qkv, grad_qv_bias, grad_dense, bias_grad, grad_up, grad_up_bias, grad_down, bias_grad)
```

```python
import functools

import jax
import jax.numpy as jnp
from jax import lax
from jax.experimental import pallas as pl
from jax.experimental.pallas import tpu as pltpu
from jax.sharding import PartitionSpec as P

D = 768
HD = 64
ROT = 16
EPS = 1e-05
NEG = -1e30
MESH = pl.DeviceIdType.MESH
F32, BF16 = jnp.float32, jnp.bfloat16
NN = (((1,), (0,)), ((), ()))
NT = (((1,), (1,)), ((), ()))
TN = (((0,), (0,)), ((), ()))


def dot(lhs, rhs, dims=NN):
    return lax.dot_general(lhs, rhs, dims, preferred_element_type=F32)


def gelu_parts(u):
    cumulative = 0.5 * (1.0 + lax.erf(u * 0.7071067811865476))
    density = jnp.exp(-0.5 * u * u) * 0.3989422804014327
    return cumulative, density


def rotate_rows(x, cos, sin):
    half = ROT // 2
    lo, hi = x[:half], x[half:ROT]
    return jnp.concatenate([lo * cos - hi * sin, hi * cos + lo * sin, x[ROT:]], axis=0)


def layer_kernel(
    n,
    heads,
    x_ref,
    c_ref,
    first_ref,
    cos_ref,
    sin_ref,
    gains_ref,
    wqkv_ref,
    qvb_ref,
    dense_ref,
    up_ref,
    upb_ref,
    down_ref,
    out_ref,
    gin_ref,
    fin,
    small_ref,
    xg,
    cg,
    hat,
    attn_in,
    mlp_in,
    kv,
    q_t,
    g_t,
    q_pad,
    g_pad,
    act,
    gpl,
    branch,
    fmax,
    fsum,
    facc,
    att_t,
    delta,
    dkv,
    dkx,
    dkz,
    gp_t,
    grads,
    from_outer,
    from_mid,
    from_x,
    parts_core,
    parts_y,
    pair_sum,
    parts_own,
    vec,
    vec_x,
    vec_pair,
    vec_z,
    vec_ctx,
    vec_tp,
    tg_send,
    tg_recv,
    tf_send,
    kv_up_send,
    kv_x_send,
    kv_recv,
    dx_send,
    dx_recv,
    dz_send,
    dz_recv,
    ar_o_send,
    ar_o_recv,
    ar_m_send,
    ar_m_recv,
    ar_x_send,
    ar_x_recv,
    fin_send,
    fin_recv,
    pc_send,
    pc_recv,
    py_send,
    py_recv,
    vx_send,
    vx_recv,
    vz_send,
    vz_recv,
    vt_send,
    vt_recv,
):
    m = n // 2
    c = lax.axis_index("ctx")
    t = lax.axis_index("tp")
    a, b = c // 2, c % 2
    core, yy = t % 2, t // 2
    sib = yy * 2 + (1 - core)
    peer = (1 - yy) * 2 + core
    diag = (1 - yy) * 2 + (1 - core)
    xp = 2 * a + (1 - b)
    low_mid, high_mid = m // 2 - 1, m // 2
    is_low = a <= low_mid
    is_mid = (a == low_mid) | (a == high_mid)
    is_end = (a == 0) | (a == m - 1)
    half = jnp.where(is_low, 0, 1)
    inner_a = jnp.where(is_low, a + 1, a - 1)
    outer_a = jnp.where(is_low, jnp.maximum(a - 1, 0), jnp.minimum(a + 1, m - 1))
    inner = (2 * inner_a + b, t)
    outer = (2 * outer_a + b, t)
    rows = hat.shape[0]
    parts = (act, xg, gpl)
    own = x_ref.shape[0]

    def copy(src, dst, send, recv, dev):
        return pltpu.make_async_remote_copy(
            src_ref=src, dst_ref=dst, send_sem=send, recv_sem=recv, device_id=dev, device_id_type=MESH
        )

    barrier = pltpu.get_barrier_semaphore()
    for dev in ((c, sib), (c, peer), (c, diag), (xp, t)):
        pl.semaphore_signal(barrier, inc=1, device_id=dev, device_id_type=MESH)
    for k in range(1, m):
        pl.semaphore_signal(
            barrier, inc=1, device_id=(2 * ((a + k) % m) + b, t), device_id_type=MESH
        )
    pl.semaphore_wait(barrier, 4 + m - 1)

    for i, (src, dst) in enumerate(((x_ref, xg), (c_ref, cg))):
        copy(src, dst.at[t], tg_send.at[i, 0], tg_recv.at[i, t], (c, peer)).start()
        copy(src, dst.at[t], tg_send.at[i, 1], tg_recv.at[i, t], (c, sib)).start()
    xg[t] = x_ref[...]
    cg[t] = c_ref[...]

    gain1, shift1 = gains_ref[0:1, :], gains_ref[1:2, :]
    gain2, shift2 = gains_ref[2:3, :], gains_ref[3:4, :]

    def norm_block(r):
        x = xg[r].astype(F32)
        mean = jnp.mean(x, axis=1, keepdims=True)
        cen = x - mean
        var = jnp.mean(cen * cen, axis=1, keepdims=True)
        inv = lax.rsqrt(var + EPS)
        h = cen * inv
        where = pl.ds(pl.multiple_of(r * own, own), own)
        hat[where, :] = h
        attn_in[where, :] = (h * gain1 + shift1).astype(BF16)
        mlp_in[where, :] = (h * gain2 + shift2).astype(BF16)

    def tg_wait(i, dst, blk):
        copy(dst.at[blk], dst.at[blk], tg_send.at[i, 0], tg_recv.at[i, blk], (c, sib)).wait_recv()

    norm_block(t)
    tg_wait(0, xg, sib)
    norm_block(sib)
    tg_wait(0, xg, peer)
    copy(xg.at[peer], xg.at[peer], tf_send.at[0], tg_recv.at[0, peer], (c, sib)).start()
    norm_block(peer)
    tg_wait(0, xg, diag)
    norm_block(diag)

    width = heads * HD
    cos, sin = cos_ref[...], sin_ref[...]
    zeros = jnp.zeros((HD, rows), F32)
    x_all = attn_in[...]
    k_t = dot(wqkv_ref[width : 2 * width, :], x_all, NT)
    v_t = dot(wqkv_ref[2 * width :, :], x_all, NT) + qvb_ref[width:, :]
    for h in range(heads):
        kh = rotate_rows(k_t[h * HD : (h + 1) * HD], cos, sin)
        kv[c, h] = jnp.concatenate([kh, v_t[h * HD : (h + 1) * HD]], axis=0).astype(BF16)

    def kv_start_own():
        @pl.when(a < m - 1)
        def _():
            copy(kv.at[c], kv.at[c], kv_up_send.at[c], kv_recv.at[c], (c + 2, t)).start()

        @pl.when(b == 0)
        def _():
            copy(kv.at[c], kv.at[c], kv_x_send.at[c], kv_recv.at[c], (xp, t)).start()

    def kv_wait(j):
        copy(kv.at[j], kv.at[j], kv_up_send.at[j], kv_recv.at[j], (xp, t)).wait_recv()

    def kv_forward(j):
        kv_wait(j)

        @pl.when(a < m - 1)
        def _():
            copy(kv.at[j], kv.at[j], kv_up_send.at[j], kv_recv.at[j], (c + 2, t)).start()

        copy(kv.at[j], kv.at[j], kv_x_send.at[j], kv_recv.at[j], (xp, t)).start()

    kv_start_own()

    tg_wait(1, cg, peer)
    copy(cg.at[peer], cg.at[peer], tf_send.at[1], tg_recv.at[1, peer], (c, sib)).start()

    q_all = dot(wqkv_ref[0:width, :], x_all, NT) + qvb_ref[0:width, :]
    for h in range(heads):
        qh = rotate_rows(q_all[h * HD : (h + 1) * HD], cos, sin).astype(BF16).astype(F32) * (HD ** -0.5)
        q_t[h] = qh.astype(BF16)
        q_pad[h] = jnp.transpose(jnp.concatenate([qh, zeros], axis=0)).astype(BF16)
    tg_wait(1, cg, sib)
    tg_wait(1, cg, diag)
    cot = cg[...].reshape(rows, D)
    ga = dot(dense_ref[...], cot, NT)
    for h in range(heads):
        gh = ga[h * HD : (h + 1) * HD].astype(BF16)
        g_t[h] = gh
        g_pad[h] = jnp.transpose(jnp.concatenate([zeros, gh.astype(F32)], axis=0)).astype(BF16)

    vec[...] = jnp.zeros_like(vec)
    copy(xg.at[peer], xg.at[peer], tf_send.at[0], tg_recv.at[0, peer], (c, sib)).wait_send()
    step = 256
    for i in range(rows // step):
        where = pl.ds(i * step, step)
        blocks = slice(i * step // own, (i + 1) * step // own)
        mi = mlp_in[where, :]
        ct = cg[blocks].reshape(step, D)
        pre = dot(mi, up_ref[...]) + upb_ref[...]
        cum, den = gelu_parts(pre)
        ac = (pre * cum).astype(BF16)
        act[blocks] = ac.reshape(-1, own, D)
        branch[where, :] = dot(ac, down_ref[...])
        gp = dot(ct, down_ref[...], NT) * (cum + pre * den)
        vec[5:6, :] += jnp.sum(gp, axis=0, keepdims=True)
        gl = gp.astype(BF16)
        gpl[blocks] = gl.reshape(-1, own, D)
        gm = dot(gl, up_ref[...], NT)
        parts[1][blocks] = gm.astype(BF16).reshape(-1, own, D)
        vec[2:3, :] += jnp.sum(gm * hat[where, :], axis=0, keepdims=True)
        vec[3:4, :] += jnp.sum(gm, axis=0, keepdims=True)
    vec[4:5, :] = jnp.sum(c_ref[...].astype(F32), axis=0, keepdims=True)

    def ar_start(s):
        @pl.when(is_end)
        def _():
            copy(grads.at[s], from_outer.at[s], ar_o_send.at[s], ar_o_recv.at[s], inner).start()

    hrows = D // 2
    qrows = D // 4
    mine_half = pl.ds(pl.multiple_of(half * hrows, hrows), hrows)
    other_half = pl.ds(pl.multiple_of((1 - half) * hrows, hrows), hrows)

    def quarter(k):
        return pl.ds(pl.multiple_of(k * qrows, qrows), qrows)

    k_own = 2 * half + b
    k_x = 2 * half + 1 - b

    def ar_a(s):
        @pl.when(jnp.logical_not(is_end))
        def _():
            copy(grads.at[s], from_outer.at[s], ar_o_send.at[s], ar_o_recv.at[s], inner).wait_recv()
            grads[s] = (grads[s].astype(F32) + from_outer[s].astype(F32)).astype(BF16)

            @pl.when(is_mid)
            def _():
                copy(
                    grads.at[s, other_half, :], from_mid.at[s], ar_m_send.at[s], ar_m_recv.at[s], inner
                ).start()

            @pl.when(jnp.logical_not(is_mid))
            def _():
                copy(grads.at[s], from_outer.at[s], ar_o_send.at[s], ar_o_recv.at[s], inner).start()

    def ar_b(s):
        @pl.when(is_mid)
        def _():
            copy(
                grads.at[s, other_half, :], from_mid.at[s], ar_m_send.at[s], ar_m_recv.at[s], inner
            ).wait_recv()
            grads[s, mine_half, :] = (
                grads[s, mine_half, :].astype(F32) + from_mid[s].astype(F32)
            ).astype(BF16)
            copy(
                grads.at[s, quarter(k_x), :], from_x.at[s], ar_x_send.at[s], ar_x_recv.at[s], (xp, t)
            ).start()

    def fin_copy(s, k, way, dev):
        return copy(
            fin.at[s, quarter(k), :],
            fin.at[s, quarter(k), :],
            fin_send.at[s, k, way],
            fin_recv.at[s, k],
            dev,
        )

    def ar_c(s):
        @pl.when(is_mid)
        def _():
            copy(
                grads.at[s, quarter(k_x), :], from_x.at[s], ar_x_send.at[s], ar_x_recv.at[s], (xp, t)
            ).wait_recv()
            fin[s, quarter(k_own), :] = (
                grads[s, quarter(k_own), :].astype(F32) + from_x[s].astype(F32)
            ).astype(BF16)
            fin_copy(s, k_own, 0, outer).start()
            fin_copy(s, k_own, 1, inner).start()
            fin_copy(s, k_own, 2, (xp, t)).start()

    def ar_d(s):
        @pl.when(is_mid)
        def _():
            fin_copy(s, k_x, 0, outer).wait_recv()
            fin_copy(s, k_x, 0, outer).start()
            fin_copy(s, k_x, 1, inner).start()

    def ar_e(s):
        @pl.when(is_mid)
        def _():
            for i in range(2):
                k = 2 * (1 - half) + i
                fin_copy(s, k, 0, outer).wait_recv()
                fin_copy(s, k, 0, outer).start()

        @pl.when(jnp.logical_not(is_mid))
        def _():
            for k in range(4):
                fin_copy(s, k, 0, outer).wait_recv()

                @pl.when(jnp.logical_not(is_end))
                def _():
                    fin_copy(s, k, 0, outer).start()

    def ar_end(s):
        @pl.when(is_mid)
        def _():
            copy(
                grads.at[s, other_half, :], from_mid.at[s], ar_m_send.at[s], ar_m_recv.at[s], inner
            ).wait_send()
            copy(
                grads.at[s, quarter(k_x), :], from_x.at[s], ar_x_send.at[s], ar_x_recv.at[s], (xp, t)
            ).wait_send()
            fin_copy(s, k_own, 0, outer).wait_send()
            fin_copy(s, k_own, 1, outer).wait_send()
            fin_copy(s, k_own, 2, outer).wait_send()
            fin_copy(s, k_x, 0, outer).wait_send()
            fin_copy(s, k_x, 1, outer).wait_send()
            for i in range(2):
                fin_copy(s, 2 * (1 - half) + i, 0, outer).wait_send()

        @pl.when(jnp.logical_not(is_mid))
        def _():
            copy(grads.at[s], from_outer.at[s], ar_o_send.at[s], ar_o_recv.at[s], inner).wait_send()

            @pl.when(jnp.logical_not(is_end))
            def _():
                for k in range(4):
                    fin_copy(s, k, 0, outer).wait_send()

    for i in range(3):
        cols = slice(i * 256, (i + 1) * 256)
        grads[0, cols, :] = dot(act[:, :, cols].reshape(rows, 256), cot, TN).astype(BF16)
    ar_start(0)

    @pl.when(a > 0)
    def _():
        kv_forward(c - 2)

    gpl_all = gpl[...].reshape(rows, D)
    for i in range(3):
        cols = slice(i * 256, (i + 1) * 256)
        grads[1, cols, :] = dot(mlp_in[:, cols], gpl_all, TN).astype(BF16)
    ar_start(1)

    def pc_copy(p, i):
        return copy(
            parts[p].at[2 * i + (1 - core)],
            parts_core.at[p, i],
            pc_send.at[p, i],
            pc_recv.at[p, i],
            (c, sib),
        )

    def py_copy(p):
        return copy(pair_sum.at[p], parts_y.at[p], py_send.at[p], py_recv.at[p], (c, peer))

    def tp_a(p):
        pc_copy(p, 1 - yy).start()
        pc_copy(p, yy).start()

    def tp_b(p):
        pc_copy(p, 1 - yy).wait_recv()
        pair_sum[p] = (
            parts[p][2 * (1 - yy) + core].astype(F32) + parts_core[p, 1 - yy].astype(F32)
        ).astype(BF16)
        py_copy(p).start()
        pc_copy(p, yy).wait_recv()
        parts_own[p] = parts[p][t].astype(F32) + parts_core[p, yy].astype(F32)

    def tp_c(p):
        py_copy(p).wait_recv()
        parts_own[p] += parts_y[p].astype(F32)

    tp_a(1)

    first = first_ref[...]
    key_iota = lax.broadcasted_iota(jnp.int32, (rows, rows), 0)
    query_iota = lax.broadcasted_iota(jnp.int32, (1, rows), 1)

    def scores_of(j, h, own_block):
        s = dot(kv[j, h, 0:HD, :], q_t[h], TN)
        visible = key_iota >= first - j * rows
        if own_block:
            visible &= key_iota <= query_iota
        return jnp.where(visible, s, NEG)

    def forward(j, own_block):
        for h in range(heads):
            s = scores_of(j, h, own_block)
            top = jnp.max(s, axis=0, keepdims=True)
            if not own_block:
                old = fmax[h]
                top = jnp.maximum(old, top)
            w = jnp.exp(s - top)
            total = jnp.sum(w, axis=0, keepdims=True)
            acc = dot(kv[j, h, HD:, :], w.astype(BF16))
            if not own_block:
                factor = jnp.exp(old - top)
                total += fsum[h] * factor
                acc += facc[h] * factor
            fmax[h] = top
            fsum[h] = total
            facc[h] = acc

    forward(c, True)

    @pl.when(b == 1)
    def _():
        kv_wait(c - 1)
        forward(c - 1, False)

    tp_b(1)

    def forward_pair(d, carry):
        @pl.when(d < a)
        def _():
            kv_forward(2 * (a - d - 1) + b)

        forward(2 * (a - d) + b, False)
        j = 2 * (a - d) + 1 - b
        kv_wait(j)
        forward(j, False)
        return carry

    lax.fori_loop(1, a + 1, forward_pair, 0)
    ar_a(0)
    ar_a(1)
    for h in range(heads):
        total = fsum[h]
        at = (facc[h] / total).astype(BF16)
        att_t[h * HD : (h + 1) * HD, :] = at
        delta[h] = jnp.sum(g_t[h].astype(F32) * at.astype(F32), axis=0, keepdims=True)
        fmax[h] = fmax[h] + jnp.log(total)
    att_all = att_t[...]
    parts[0][...] = (
        (branch[...] + dot(att_all, dense_ref[...], TN)).astype(BF16).reshape(-1, own, D)
    )
    tp_a(0)
    grads[2, 3 * width :, :] = dot(att_all, cot).astype(BF16)
    ar_b(0)
    ar_b(1)
    tp_c(1)

    facc[...] = jnp.zeros_like(facc)

    slots = dkv.shape[1]

    def backward(j, own_block, slot, kind):
        for h in range(heads):
            s = scores_of(j, h, own_block)
            w = jnp.exp(s - fmax[h])
            dw = dot(kv[j, h, HD:, :], g_t[h], TN)
            ds = (w * (dw - delta[h])).astype(BF16)
            dkv[kind, lax.rem(slot, slots), h] = (dot(ds, q_pad[h]) + dot(w.astype(BF16), g_pad[h])).astype(BF16)
            facc[h] += dot(kv[j, h, 0:HD, :], ds)

    def dx_copy(slot):
        return copy(
            dkv.at[0, lax.rem(slot, slots)], dkx.at[slot], dx_send.at[slot], dx_recv.at[slot], (xp, t)
        )

    def dz_copy(slot, dev):
        return copy(
            dkv.at[1, lax.rem(slot, slots)], dkz.at[slot], dz_send.at[slot], dz_recv.at[slot], dev
        )

    def reuse(slot):
        @pl.when(slot >= slots)
        def _():
            dx_copy(slot - slots).wait_send()
            dz_copy(slot - slots, (xp, t)).wait_send()

    below = (jnp.maximum(c - 2, 0), t)

    def pass_down(slot):
        where = lax.rem(slot, slots)
        dx_copy(slot).wait_recv()

        @pl.when(a < m - 1)
        def _():
            dz_copy(slot, below).wait_recv()
            for h in range(heads):
                dkv[1, where, h] = (
                    dkv[1, where, h].astype(F32) + dkx[slot, h].astype(F32) + dkz[slot, h].astype(F32)
                ).astype(BF16)

        @pl.when(a == m - 1)
        def _():
            for h in range(heads):
                dkv[1, where, h] = (dkv[1, where, h].astype(F32) + dkx[slot, h].astype(F32)).astype(BF16)

        dz_copy(slot, below).start()

    def backward_pair(slot, carry):
        reuse(slot)
        backward(2 * slot + 1 - b, False, slot, 0)
        dx_copy(slot).start()
        backward(2 * slot + b, False, slot, 1)

        @pl.when(slot > 0)
        def _():
            pass_down(slot - 1)

        return carry

    lax.fori_loop(0, a, backward_pair, 0)
    reuse(a)

    @pl.when(b == 1)
    def _():
        backward(c - 1, False, a, 0)
        dx_copy(a).start()

    @pl.when(a > 0)
    def _():
        pass_down(a - 1)

    tp_b(0)
    backward(c, True, a, 1)
    ar_c(0)
    ar_c(1)

    @pl.when(b == 0)
    def _():
        dx_copy(a).wait_recv()

    @pl.when(a < m - 1)
    def _():
        dz_copy(a, below).wait_recv()

    for h in range(heads):
        top = h * HD
        gq = rotate_rows(facc[h] * (HD ** -0.5), cos, -sin)
        own_sum = dkv[1, lax.rem(a, slots), h].astype(F32)
        own_sum += jnp.where(b == 0, dkx[a, h].astype(F32), 0.0)
        own_sum += jnp.where(a < m - 1, dkz[a, h].astype(F32), 0.0)
        own_t = jnp.transpose(own_sum)
        gk = rotate_rows(own_t[0:HD], cos, -sin)
        gv = own_t[HD:]
        gp_t[top : top + HD, :] = gq.astype(BF16)
        gp_t[width + top : width + top + HD, :] = gk.astype(BF16)
        gp_t[2 * width + top : 2 * width + top + HD, :] = gv.astype(BF16)
        both = jnp.concatenate([gq, gv], axis=0)
        lanes = both[:, 0:128]
        for i in range(1, rows // 128):
            lanes += both[:, i * 128 : (i + 1) * 128]
        vec[6:7, h * 128 : (h + 1) * 128] = jnp.sum(jnp.transpose(lanes), axis=0, keepdims=True)

    gp_all = gp_t[...]
    grads[2, 0 : 3 * width, :] = dot(gp_all, attn_in[...]).astype(BF16)
    ar_start(2)
    for i in range(rows // step):
        where = slice(i * step, (i + 1) * step)
        gat = dot(gp_all[:, where], wqkv_ref[...], TN)
        parts[2][i * step // own : (i + 1) * step // own] = gat.astype(BF16).reshape(-1, own, D)
        if i == 0:
            vec[0:1, :] = jnp.sum(gat * hat[where, :], axis=0, keepdims=True)
            vec[1:2, :] = jnp.sum(gat, axis=0, keepdims=True)
        else:
            vec[0:1, :] += jnp.sum(gat * hat[where, :], axis=0, keepdims=True)
            vec[1:2, :] += jnp.sum(gat, axis=0, keepdims=True)
    tp_a(2)

    vx = copy(vec, vec_x, vx_send, vx_recv, (xp, t))
    vx.start()
    tp_b(2)
    tp_c(0)
    ar_a(2)
    vx.wait_recv()
    vec_pair[...] = vec[...] + vec_x[...]

    def vz_copy(k):
        return copy(
            vec_pair, vec_z.at[k], vz_send.at[k], vz_recv.at[k], (2 * ((a + k + 1) % m) + b, t)
        )

    for k in range(m - 1):
        vz_copy(k).start()
    ar_d(0)
    ar_d(1)
    ar_b(2)
    total = vec_pair[...]
    for k in range(m - 1):
        vz_copy(k).wait_recv()
        total += vec_z[k]
    vec_ctx[...] = total

    def vt_copy(k, dev):
        return copy(vec_ctx, vec_tp.at[k], vt_send.at[k], vt_recv.at[k], dev)

    for k, dev in enumerate((sib, peer, diag)):
        vt_copy(k, (c, dev)).start()
    ar_c(2)
    ar_e(0)
    ar_e(1)
    ar_d(2)

    tp_c(2)
    mine = pl.ds(pl.multiple_of(t * own, own), own)
    x = x_ref[...].astype(F32)
    mean = jnp.mean(x, axis=1, keepdims=True)
    cen = x - mean
    inv = lax.rsqrt(jnp.mean(cen * cen, axis=1, keepdims=True) + EPS)
    h1 = hat[mine, :]
    out_ref[...] = (x + parts_own[0] + gains_ref[4:5, :] + gains_ref[5:6, :]).astype(BF16)

    def norm_back(dh, gain):
        gh = dh * gain
        return inv * (
            gh - jnp.mean(gh, axis=1, keepdims=True) - h1 * jnp.mean(gh * h1, axis=1, keepdims=True)
        )

    gin_ref[...] = (
        c_ref[...].astype(F32) + norm_back(parts_own[2], gain1) + norm_back(parts_own[1], gain2)
    )
    for k in range(3):
        vt_copy(k, (c, sib)).wait_recv()
    small_ref[0:5, :] = vec_ctx[0:5, :] + vec_tp[0, 0:5, :] + vec_tp[1, 0:5, :] + vec_tp[2, 0:5, :]
    small_ref[5:8, :] = vec_ctx[5:8, :]
    ar_e(2)

    for i in range(2):
        src, dst = ((x_ref, xg), (c_ref, cg))[i]
        copy(src, dst.at[t], tg_send.at[i, 0], tg_recv.at[i, t], (c, peer)).wait_send()
        copy(src, dst.at[t], tg_send.at[i, 1], tg_recv.at[i, t], (c, sib)).wait_send()

    copy(cg.at[peer], cg.at[peer], tf_send.at[1], tg_recv.at[1, peer], (c, sib)).wait_send()

    @pl.when(a < m - 1)
    def _():
        def up_done(d, carry):
            j = 2 * d + b
            copy(kv.at[j], kv.at[j], kv_up_send.at[j], kv_recv.at[j], (xp, t)).wait_send()
            return carry

        lax.fori_loop(0, a + 1, up_done, 0)

    def x_done(d, carry):
        j = 2 * d + b
        copy(kv.at[j], kv.at[j], kv_x_send.at[j], kv_recv.at[j], (xp, t)).wait_send()
        return carry

    lax.fori_loop(0, a, x_done, 0)

    def down_done(d, carry):
        dx_copy(d).wait_send()
        dz_copy(d, below).wait_send()
        return carry

    lax.fori_loop(jnp.maximum(a - slots + 1, 0), a, down_done, 0)

    @pl.when(b == 0)
    def _():
        copy(kv.at[c], kv.at[c], kv_x_send.at[c], kv_recv.at[c], (xp, t)).wait_send()

    @pl.when(b == 1)
    def _():
        dx_copy(a).wait_send()

    for p in range(3):
        pc_copy(p, 0).wait_send()
        pc_copy(p, 1).wait_send()
        py_copy(p).wait_send()
    for s in range(3):
        ar_end(s)
    vx.wait_send()
    for k in range(m - 1):
        vz_copy(k).wait_send()
    for k in range(3):
        vt_copy(k, (c, sib)).wait_send()


def layer(n, heads, own, *args):
    rows = args[2].shape[1]
    m = n // 2
    hidden = D
    vmem, dma = pltpu.VMEM, pltpu.SemaphoreType.DMA
    scratch = [
        vmem((rows // own, own, D), BF16),
        vmem((rows // own, own, D), BF16),
        vmem((rows, D), F32),
        vmem((rows, D), BF16),
        vmem((rows, D), BF16),
        vmem((n, heads, 2 * HD, rows), BF16),
        vmem((heads, HD, rows), BF16),
        vmem((heads, HD, rows), BF16),
        vmem((heads, rows, 2 * HD), BF16),
        vmem((heads, rows, 2 * HD), BF16),
        vmem((rows // own, own, hidden), BF16),
        vmem((rows // own, own, hidden), BF16),
        vmem((rows, D), F32),
        vmem((heads, 1, rows), F32),
        vmem((heads, 1, rows), F32),
        vmem((heads, HD, rows), F32),
        vmem((heads * HD, rows), BF16),
        vmem((heads, 1, rows), F32),
        vmem((2, 4 if m <= 4 else 2, heads, rows, 2 * HD), BF16),
        vmem((m, heads, rows, 2 * HD), BF16),
        vmem((m, heads, rows, 2 * HD), BF16),
        vmem((3 * heads * HD, rows), BF16),
        vmem((3, D, D), BF16),
        vmem((3, D, D), BF16),
        vmem((3, D // 2, D), BF16),
        vmem((3, D // 4, D), BF16),
        vmem((3, 2, own, D), BF16),
        vmem((3, own, D), BF16),
        vmem((3, own, D), BF16),
        vmem((3, own, D), F32),
        vmem((8, D), F32),
        vmem((8, D), F32),
        vmem((8, D), F32),
        vmem((m - 1, 8, D), F32),
        vmem((8, D), F32),
        vmem((3, 8, D), F32),
        dma((2, 2)),
        dma((2, 4)),
        dma((2,)),
        dma((n,)),
        dma((n,)),
        dma((n,)),
        dma((m,)),
        dma((m,)),
        dma((m,)),
        dma((m,)),
        dma((3,)),
        dma((3,)),
        dma((3,)),
        dma((3,)),
        dma((3,)),
        dma((3,)),
        dma((3, 4, 3)),
        dma((3, 4)),
        dma((3, 2)),
        dma((3, 2)),
        dma((3,)),
        dma((3,)),
        dma(()),
        dma(()),
        dma((m - 1,)),
        dma((m - 1,)),
        dma((3,)),
        dma((3,)),
    ]
    return pl.pallas_call(
        functools.partial(layer_kernel, n, heads),
        out_shape=[
            jax.ShapeDtypeStruct((own, D), BF16),
            jax.ShapeDtypeStruct((own, D), F32),
            jax.ShapeDtypeStruct((3, D, D), BF16),
            jax.ShapeDtypeStruct((8, D), F32),
        ],
        in_specs=[pl.BlockSpec(memory_space=pltpu.VMEM)] * 12,
        out_specs=[pl.BlockSpec(memory_space=pltpu.VMEM)] * 4,
        scratch_shapes=scratch,
        compiler_params=pltpu.CompilerParams(
            collective_id=1, has_side_effects=True, vmem_limit_bytes=62 * 1024 * 1024
        ),
        name="layer",
    )(*args)


def local(
    inputs,
    positions,
    attn_scale,
    attn_shift,
    mlp_scale,
    mlp_shift,
    qkv_weight,
    qv_bias,
    dense_weight,
    dense_bias,
    up_weight,
    up_bias,
    down_weight,
    down_bias,
    cotangent,
):
    width = qkv_weight.shape[2]
    heads = width // HD
    rows = positions.shape[0]
    n = lax.axis_size("ctx")
    ctx_index = lax.axis_index("ctx")
    freqs = 10000.0 ** (-jnp.arange(0, ROT, 2).astype(F32) / ROT)
    angles = freqs[:, None] * positions.astype(F32)[None, :]
    first = (ctx_index * rows + jnp.arange(rows, dtype=jnp.int32) - positions)[None, :]
    zero = jnp.zeros_like(dense_bias)
    gains = jnp.stack(
        [attn_scale, attn_shift, mlp_scale, mlp_shift, dense_bias, down_bias, zero, zero]
    )
    wqkv = jnp.transpose(qkv_weight, (1, 2, 0)).reshape(3 * width, D)
    output, grad_input, fin, small = layer(
        n,
        heads,
        inputs.shape[0],
        inputs,
        cotangent,
        first,
        jnp.cos(angles),
        jnp.sin(angles),
        gains,
        wqkv,
        qv_bias.reshape(2 * width, 1),
        dense_weight,
        up_weight,
        up_bias[None, :],
        down_weight,
    )
    grad_qkv = jnp.transpose(fin[2, : 3 * width].astype(F32).reshape(3, width, D), (2, 0, 1))
    qv = small[6, : 2 * width].reshape(heads, 2, HD)
    return (
        output,
        grad_input,
        small[0],
        small[1],
        small[2],
        small[3],
        grad_qkv,
        jnp.transpose(qv, (1, 0, 2)).reshape(2, width),
        fin[2, 3 * width :].astype(F32),
        small[4],
        fin[1].astype(F32),
        small[5],
        fin[0].astype(F32),
        small[4],
    )


def solution(mesh):
    in_specs = (
        P(("ctx", "tp"), None),
        P("ctx"),
        P(),
        P(),
        P(),
        P(),
        P(None, None, "tp"),
        P(None, "tp"),
        P("tp", None),
        P(),
        P(None, "tp"),
        P("tp"),
        P("tp", None),
        P(),
        P(("ctx", "tp"), None),
    )
    out_specs = (
        P(("ctx", "tp"), None),
        P(("ctx", "tp"), None),
        P(),
        P(),
        P(),
        P(),
        P(None, None, "tp"),
        P(None, "tp"),
        P("tp", None),
        P(),
        P(None, "tp"),
        P("tp"),
        P("tp", None),
        P(),
    )
    return jax.shard_map(local, mesh=mesh, in_specs=in_specs, out_specs=out_specs, check_vma=False)
```

```python
import functools

import jax
import jax.numpy as jnp
from jax import lax
from jax.experimental import pallas as pl
from jax.experimental.pallas import tpu as pltpu
from jax.sharding import PartitionSpec as P

D = 768
HD = 64
ROT = 16
EPS = 1e-05
NEG = -1e30
MESH = pl.DeviceIdType.MESH
F32, BF16 = jnp.float32, jnp.bfloat16
NN = (((1,), (0,)), ((), ()))
NT = (((1,), (1,)), ((), ()))
TN = (((0,), (0,)), ((), ()))
SEGMENTS = ((0, 384), (384, 384), (768, 384), (1152, 384), (1536, 384), (1920, 192), (2112, 192))
ROWS = 2304


def dot(lhs, rhs, dims=NN):
    return lax.dot_general(lhs, rhs, dims, preferred_element_type=F32)


def gelu_parts(u):
    cumulative = 0.5 * (1.0 + lax.erf(u * 0.7071067811865476))
    density = jnp.exp(-0.5 * u * u) * 0.3989422804014327
    return cumulative, density


def rotate_rows(x, cos, sin):
    half = ROT // 2
    lo, hi = x[:half], x[half:ROT]
    return jnp.concatenate([lo * cos - hi * sin, hi * cos + lo * sin, x[ROT:]], axis=0)


def layer_kernel(
    n,
    heads,
    x_ref,
    c_ref,
    pos_ref,
    gain1_ref,
    shift1_ref,
    gain2_ref,
    shift2_ref,
    denseb_ref,
    downb_ref,
    wqkv_ref,
    qvb_ref,
    dense_ref,
    up_ref,
    upb_ref,
    down_ref,
    out_ref,
    gin_ref,
    fin,
    small_ref,
    xg,
    cg,
    hat,
    attn_in,
    mlp_in,
    kv,
    q_t,
    g_t,
    q_pad,
    g_pad,
    act,
    gpl,
    branch,
    fmax,
    fsum,
    facc,
    att_t,
    delta,
    dkv,
    dkx,
    dkz,
    gp_t,
    grads,
    from_outer,
    from_mid,
    from_x,
    parts_core,
    parts_y,
    pair_sum,
    parts_own,
    vec,
    vec_x,
    vec_pair,
    vec_z,
    vec_ctx,
    vec_tp,
    tg_send,
    tg_recv,
    tf_send,
    kv_up_send,
    kv_x_send,
    kv_recv,
    dx_send,
    dx_recv,
    dz_send,
    dz_recv,
    ar_o_send,
    ar_o_recv,
    ar_m_send,
    ar_m_recv,
    ar_x_send,
    ar_x_recv,
    fin_send,
    fin_recv,
    pc_send,
    pc_recv,
    py_send,
    py_recv,
    vx_send,
    vx_recv,
    vz_send,
    vz_recv,
    vt_send,
    vt_recv,
):
    m = n // 2
    c = lax.axis_index("ctx")
    t = lax.axis_index("tp")
    a, b = c // 2, c % 2
    core, yy = t % 2, t // 2
    sib = yy * 2 + (1 - core)
    peer = (1 - yy) * 2 + core
    diag = (1 - yy) * 2 + (1 - core)
    xp = 2 * a + (1 - b)
    low_mid, high_mid = m // 2 - 1, m // 2
    is_low = a <= low_mid
    is_mid = (a == low_mid) | (a == high_mid)
    is_end = (a == 0) | (a == m - 1)
    half = jnp.where(is_low, 0, 1)
    inner_a = jnp.where(is_low, a + 1, a - 1)
    outer_a = jnp.where(is_low, jnp.maximum(a - 1, 0), jnp.minimum(a + 1, m - 1))
    inner = (2 * inner_a + b, t)
    outer = (2 * outer_a + b, t)
    rows = hat.shape[0]
    parts = (act, xg, gpl)
    own = x_ref.shape[0]

    def copy(src, dst, send, recv, dev):
        return pltpu.make_async_remote_copy(
            src_ref=src, dst_ref=dst, send_sem=send, recv_sem=recv, device_id=dev, device_id_type=MESH
        )

    barrier = pltpu.get_barrier_semaphore()
    for dev in ((c, sib), (c, peer), (c, diag), (xp, t)):
        pl.semaphore_signal(barrier, inc=1, device_id=dev, device_id_type=MESH)
    for k in range(1, m):
        pl.semaphore_signal(
            barrier, inc=1, device_id=(2 * ((a + k) % m) + b, t), device_id_type=MESH
        )
    pl.semaphore_wait(barrier, 4 + m - 1)

    for i, (src, dst) in enumerate(((x_ref, xg), (c_ref, cg))):
        copy(src, dst.at[t], tg_send.at[i, 0], tg_recv.at[i, t], (c, peer)).start()
        copy(src, dst.at[t], tg_send.at[i, 1], tg_recv.at[i, t], (c, sib)).start()
    xg[t] = x_ref[...]
    cg[t] = c_ref[...]

    def as_row(ref):
        return ref[...].reshape(1, -1)

    gain1, shift1, gain2, shift2 = map(as_row, (gain1_ref, shift1_ref, gain2_ref, shift2_ref))
    positions = as_row(pos_ref)
    freqs = jnp.zeros((ROT // 2, rows), F32)
    which = lax.broadcasted_iota(jnp.int32, (ROT // 2, rows), 0)
    for i in range(ROT // 2):
        freqs = jnp.where(which == i, float(10000.0 ** (-2.0 * i / ROT)), freqs)
    angles = freqs * positions.astype(F32)
    cos, sin = jnp.cos(angles), jnp.sin(angles)
    first = c * rows + lax.broadcasted_iota(jnp.int32, (1, rows), 1) - positions

    def norm_block(r):
        x = xg[r].astype(F32)
        mean = jnp.mean(x, axis=1, keepdims=True)
        cen = x - mean
        var = jnp.mean(cen * cen, axis=1, keepdims=True)
        inv = lax.rsqrt(var + EPS)
        h = cen * inv
        where = pl.ds(pl.multiple_of(r * own, own), own)
        hat[where, :] = h
        attn_in[where, :] = (h * gain1 + shift1).astype(BF16)
        mlp_in[where, :] = (h * gain2 + shift2).astype(BF16)

    def tg_wait(i, dst, blk):
        copy(dst.at[blk], dst.at[blk], tg_send.at[i, 0], tg_recv.at[i, blk], (c, sib)).wait_recv()

    norm_block(t)
    tg_wait(0, xg, sib)
    norm_block(sib)
    tg_wait(0, xg, peer)
    copy(xg.at[peer], xg.at[peer], tf_send.at[0], tg_recv.at[0, peer], (c, sib)).start()
    norm_block(peer)
    tg_wait(0, xg, diag)
    norm_block(diag)

    width = heads * HD

    def as_column(row):
        count = row.shape[1]
        same = lax.broadcasted_iota(jnp.int32, (count, count), 0) == lax.broadcasted_iota(
            jnp.int32, (count, count), 1
        )
        return jnp.sum(jnp.where(same, row, 0.0), axis=1, keepdims=True)

    zeros = jnp.zeros((HD, rows), F32)
    x_all = attn_in[...]
    k_t = dot(wqkv_ref[width : 2 * width, :], x_all, NT)
    v_t = dot(wqkv_ref[2 * width :, :], x_all, NT) + as_column(qvb_ref[1:2, :])
    for h in range(heads):
        kh = rotate_rows(k_t[h * HD : (h + 1) * HD], cos, sin)
        kv[c, h] = jnp.concatenate([kh, v_t[h * HD : (h + 1) * HD]], axis=0).astype(BF16)

    def kv_start_own():
        @pl.when(a < m - 1)
        def _():
            copy(kv.at[c], kv.at[c], kv_up_send.at[c], kv_recv.at[c], (c + 2, t)).start()

        @pl.when(b == 0)
        def _():
            copy(kv.at[c], kv.at[c], kv_x_send.at[c], kv_recv.at[c], (xp, t)).start()

    def kv_wait(j):
        copy(kv.at[j], kv.at[j], kv_up_send.at[j], kv_recv.at[j], (xp, t)).wait_recv()

    def kv_forward(j):
        kv_wait(j)

        @pl.when(a < m - 1)
        def _():
            copy(kv.at[j], kv.at[j], kv_up_send.at[j], kv_recv.at[j], (c + 2, t)).start()

        copy(kv.at[j], kv.at[j], kv_x_send.at[j], kv_recv.at[j], (xp, t)).start()

    kv_start_own()

    tg_wait(1, cg, peer)
    copy(cg.at[peer], cg.at[peer], tf_send.at[1], tg_recv.at[1, peer], (c, sib)).start()

    q_all = dot(wqkv_ref[0:width, :], x_all, NT) + as_column(qvb_ref[0:1, :])
    for h in range(heads):
        qh = rotate_rows(q_all[h * HD : (h + 1) * HD], cos, sin).astype(BF16).astype(F32) * (HD ** -0.5)
        q_t[h] = qh.astype(BF16)
        q_pad[h] = jnp.transpose(jnp.concatenate([qh, zeros], axis=0)).astype(BF16)
    tg_wait(1, cg, sib)
    tg_wait(1, cg, diag)
    cot = cg[...].reshape(rows, D)
    ga = dot(dense_ref[...], cot, NT)
    for h in range(heads):
        gh = ga[h * HD : (h + 1) * HD].astype(BF16)
        g_t[h] = gh
        g_pad[h] = jnp.transpose(jnp.concatenate([zeros, gh.astype(F32)], axis=0)).astype(BF16)

    vec[...] = jnp.zeros_like(vec)
    copy(xg.at[peer], xg.at[peer], tf_send.at[0], tg_recv.at[0, peer], (c, sib)).wait_send()
    step = 256
    for i in range(rows // step):
        where = pl.ds(i * step, step)
        blocks = slice(i * step // own, (i + 1) * step // own)
        mi = mlp_in[where, :]
        ct = cg[blocks].reshape(step, D)
        pre = dot(mi, up_ref[...]) + as_row(upb_ref)
        cum, den = gelu_parts(pre)
        ac = (pre * cum).astype(BF16)
        act[blocks] = ac.reshape(-1, own, D)
        branch[where, :] = dot(ac, down_ref[...])
        gp = dot(ct, down_ref[...], NT) * (cum + pre * den)
        vec[5:6, :] += jnp.sum(gp, axis=0, keepdims=True)
        gl = gp.astype(BF16)
        gpl[blocks] = gl.reshape(-1, own, D)
        gm = dot(gl, up_ref[...], NT)
        parts[1][blocks] = gm.astype(BF16).reshape(-1, own, D)
        vec[2:3, :] += jnp.sum(gm * hat[where, :], axis=0, keepdims=True)
        vec[3:4, :] += jnp.sum(gm, axis=0, keepdims=True)
    vec[4:5, :] = jnp.sum(c_ref[...].astype(F32), axis=0, keepdims=True)

    k_own = 2 * half + b
    k_x = 2 * half + 1 - b

    def part(seg, k, count, shrink=1):
        off, size = SEGMENTS[seg]
        piece = size // count
        return pl.ds(pl.multiple_of(off // shrink + k * piece, 16), piece)

    def outer_copy(i):
        where = part(i, 0, 1)
        return copy(grads.at[where], from_outer.at[where], ar_o_send.at[i], ar_o_recv.at[i], inner)

    def mid_copy(i):
        return copy(
            grads.at[part(i, 1 - half, 2)],
            from_mid.at[pl.ds(SEGMENTS[i][0] // 2, SEGMENTS[i][1] // 2)],
            ar_m_send.at[i],
            ar_m_recv.at[i],
            inner,
        )

    def x_copy(i):
        return copy(
            grads.at[part(i, k_x, 4)],
            from_x.at[pl.ds(SEGMENTS[i][0] // 4, SEGMENTS[i][1] // 4)],
            ar_x_send.at[i],
            ar_x_recv.at[i],
            (xp, t),
        )

    def fin_copy(i, k, way, dev):
        where = part(i, k, 4)
        return copy(fin.at[where], fin.at[where], fin_send.at[i, k, way], fin_recv.at[i, k], dev)

    def ar_start(i, where=True):
        @pl.when(is_end & where)
        def _():
            if i:
                outer_copy(i - 1).wait_send()
            outer_copy(i).start()

    def ar_a(i):
        @pl.when(jnp.logical_not(is_end))
        def _():
            outer_copy(i).wait_recv()
            where = part(i, 0, 1)
            grads[where, :] = (grads[where, :].astype(F32) + from_outer[where, :].astype(F32)).astype(BF16)

            @pl.when(is_mid)
            def _():
                mid_copy(i).start()

            @pl.when(jnp.logical_not(is_mid))
            def _():
                outer_copy(i).start()

    def ar_b(i):
        @pl.when(is_mid)
        def _():
            mid_copy(i).wait_recv()
            where = part(i, half, 2)
            grads[where, :] = (
                grads[where, :].astype(F32)
                + from_mid[SEGMENTS[i][0] // 2 : sum(SEGMENTS[i]) // 2, :].astype(F32)
            ).astype(BF16)
            x_copy(i).start()

    def ar_c(i):
        @pl.when(is_mid)
        def _():
            x_copy(i).wait_recv()
            where = part(i, k_own, 4)
            fin[where, :] = (
                grads[where, :].astype(F32)
                + from_x[SEGMENTS[i][0] // 4 : sum(SEGMENTS[i]) // 4, :].astype(F32)
            ).astype(BF16)
            fin_copy(i, k_own, 2, (xp, t)).start()
            fin_copy(i, k_own, 1, inner).start()
            fin_copy(i, k_own, 0, outer).start()

    k_in = 2 * (1 - half) + b

    def ar_e(i):
        @pl.when(is_mid)
        def _():
            fin_copy(i, k_in, 0, outer).wait_recv()
            fin_copy(i, k_in, 2, (xp, t)).start()
            fin_copy(i, k_in, 0, outer).start()

    def ar_f(i):
        @pl.when(jnp.logical_not(is_mid))
        def _():
            for k in range(2):
                fin_copy(i, 2 * k + b, 0, outer).wait_recv()
                fin_copy(i, 2 * k + b, 2, (xp, t)).start()

                @pl.when(jnp.logical_not(is_end))
                def _():
                    fin_copy(i, 2 * k + b, 0, outer).start()

    def ar_far(i):
        for k in range(2):
            fin_copy(i, 2 * k + 1 - b, 0, outer).wait_recv()

    def ar_end(i):
        @pl.when(is_mid)
        def _():
            mid_copy(i).wait_send()
            x_copy(i).wait_send()
            for way in range(3):
                fin_copy(i, k_own, way, outer).wait_send()
            fin_copy(i, k_in, 0, outer).wait_send()
            fin_copy(i, k_in, 2, outer).wait_send()

        @pl.when(jnp.logical_not(is_mid))
        def _():
            if i == len(SEGMENTS) - 1:
                outer_copy(i).wait_send()
            else:

                @pl.when(jnp.logical_not(is_end))
                def _():
                    outer_copy(i).wait_send()

            for k in range(2):
                fin_copy(i, 2 * k + b, 2, outer).wait_send()

                @pl.when(jnp.logical_not(is_end))
                def _():
                    fin_copy(i, 2 * k + b, 0, outer).wait_send()

    def ar_steps(*steps):
        table = dict(a=ar_a, b=ar_b, c=ar_c, e=ar_e, f=ar_f)
        for name in steps:
            table[name[0]](int(name[1:]))

    for i in range(2):
        cols = slice(i * 384, (i + 1) * 384)
        grads[i * 384 : (i + 1) * 384, :] = dot(act[:, :, cols].reshape(rows, 384), cot, TN).astype(BF16)
    ar_start(0)

    @pl.when(a > 0)
    def _():
        kv_forward(c - 2)

    gpl_all = gpl[...].reshape(rows, D)
    for i in range(2):
        cols = slice(i * 384, (i + 1) * 384)
        grads[D + i * 384 : D + (i + 1) * 384, :] = dot(mlp_in[:, cols], gpl_all, TN).astype(BF16)
    for i in range(1, 4):
        ar_start(i, a == 0)

    def pc_copy(p, i):
        return copy(
            parts[p].at[2 * i + (1 - core)],
            parts_core.at[p, i],
            pc_send.at[p, i],
            pc_recv.at[p, i],
            (c, sib),
        )

    def py_copy(p):
        return copy(pair_sum.at[p], parts_y.at[p], py_send.at[p], py_recv.at[p], (c, peer))

    def tp_a(p):
        pc_copy(p, 1 - yy).start()
        pc_copy(p, yy).start()

    def tp_b(p):
        pc_copy(p, 1 - yy).wait_recv()
        pair_sum[p] = (
            parts[p][2 * (1 - yy) + core].astype(F32) + parts_core[p, 1 - yy].astype(F32)
        ).astype(BF16)
        py_copy(p).start()
        pc_copy(p, yy).wait_recv()
        parts_own[p] = parts[p][t].astype(F32) + parts_core[p, yy].astype(F32)

    def tp_c(p):
        py_copy(p).wait_recv()
        parts_own[p] += parts_y[p].astype(F32)

    tp_a(1)

    key_iota = lax.broadcasted_iota(jnp.int32, (rows, rows), 0)
    query_iota = lax.broadcasted_iota(jnp.int32, (1, rows), 1)

    def scores_of(j, h, own_block):
        s = dot(kv[j, h, 0:HD, :], q_t[h], TN)
        visible = key_iota >= first - j * rows
        if own_block:
            visible &= key_iota <= query_iota
        return jnp.where(visible, s, NEG)

    def forward(j, own_block):
        for h in range(heads):
            s = scores_of(j, h, own_block)
            top = jnp.max(s, axis=0, keepdims=True)
            if not own_block:
                old = fmax[h]
                top = jnp.maximum(old, top)
            w = jnp.exp(s - top)
            total = jnp.sum(w, axis=0, keepdims=True)
            acc = dot(kv[j, h, HD:, :], w.astype(BF16))
            if not own_block:
                factor = jnp.exp(old - top)
                total += fsum[h] * factor
                acc += facc[h] * factor
            fmax[h] = top
            fsum[h] = total
            facc[h] = acc

    forward(c, True)

    @pl.when(b == 1)
    def _():
        kv_wait(c - 1)
        forward(c - 1, False)

    tp_b(1)

    def forward_pair(d, carry):
        @pl.when(d < a)
        def _():
            kv_forward(2 * (a - d - 1) + b)

        forward(2 * (a - d) + b, False)
        j = 2 * (a - d) + 1 - b
        kv_wait(j)
        forward(j, False)
        ar_start(1, (a > 0) & (d == 1))
        return carry

    lax.fori_loop(1, a + 1, forward_pair, 0)
    ar_start(2, a > 0)
    for h in range(heads):
        total = fsum[h]
        at = (facc[h] / total).astype(BF16)
        att_t[h * HD : (h + 1) * HD, :] = at
        delta[h] = jnp.sum(g_t[h].astype(F32) * at.astype(F32), axis=0, keepdims=True)
        fmax[h] = fmax[h] + jnp.log(total)
    att_all = att_t[...]
    parts[0][...] = (
        (branch[...] + dot(att_all, dense_ref[...], TN)).astype(BF16).reshape(-1, own, D)
    )
    tp_a(0)
    grads[2 * D : 2 * D + width, :] = dot(att_all, cot).astype(BF16)
    ar_steps("a0", "b0", "a1", "c0")

    def add_bias_sums(x, row, h):
        lanes = x[:, 0:128]
        for i in range(1, rows // 128):
            lanes += x[:, i * 128 : (i + 1) * 128]
        vec[row : row + 1, h * HD : (h + 1) * HD] = jnp.sum(jnp.transpose(lanes), axis=0, keepdims=True)

    facc[...] = jnp.zeros_like(facc)

    slots = dkv.shape[1]

    def backward(j, own_block, slot, kind):
        for h in range(heads):
            s = scores_of(j, h, own_block)
            w = jnp.exp(s - fmax[h])
            dw = dot(kv[j, h, HD:, :], g_t[h], TN)
            ds = (w * (dw - delta[h])).astype(BF16)
            dkv[kind, lax.rem(slot, slots), h] = (dot(ds, q_pad[h]) + dot(w.astype(BF16), g_pad[h])).astype(BF16)
            facc[h] += dot(kv[j, h, 0:HD, :], ds)

    def dx_copy(slot):
        return copy(
            dkv.at[0, lax.rem(slot, slots)], dkx.at[slot], dx_send.at[slot], dx_recv.at[slot], (xp, t)
        )

    def dz_copy(slot, dev):
        return copy(
            dkv.at[1, lax.rem(slot, slots)], dkz.at[slot], dz_send.at[slot], dz_recv.at[slot], dev
        )

    def reuse(slot):
        @pl.when(slot >= slots)
        def _():
            dx_copy(slot - slots).wait_send()
            dz_copy(slot - slots, (xp, t)).wait_send()

    below = (jnp.maximum(c - 2, 0), t)

    def pass_down(slot):
        where = lax.rem(slot, slots)
        dx_copy(slot).wait_recv()

        @pl.when(a < m - 1)
        def _():
            dz_copy(slot, below).wait_recv()
            for h in range(heads):
                dkv[1, where, h] = (
                    dkv[1, where, h].astype(F32) + dkx[slot, h].astype(F32) + dkz[slot, h].astype(F32)
                ).astype(BF16)

        @pl.when(a == m - 1)
        def _():
            for h in range(heads):
                dkv[1, where, h] = (dkv[1, where, h].astype(F32) + dkx[slot, h].astype(F32)).astype(BF16)

        dz_copy(slot, below).start()

    def backward_pair(slot, carry):
        reuse(slot)
        backward(2 * slot + 1 - b, False, slot, 0)
        dx_copy(slot).start()
        backward(2 * slot + b, False, slot, 1)

        @pl.when(jnp.logical_and(slot > 0, early))
        def _():
            pass_down(slot - 1)

        ar_start(3, (a > 0) & (slot == 1))
        return carry

    early = jnp.logical_or(a == m - 1, m > 4)
    lax.fori_loop(0, a, backward_pair, 0)
    reuse(a)

    @pl.when(b == 1)
    def _():
        backward(c - 1, False, a, 0)
        dx_copy(a).start()

    @pl.when(jnp.logical_and(a > 0, early))
    def _():
        pass_down(a - 1)

    backward(c, True, a, 1)
    tp_b(0)
    tp_c(1)
    for h in range(heads):
        gq = rotate_rows(facc[h] * (HD ** -0.5), cos, -sin)
        gp_t[h * HD : (h + 1) * HD, :] = gq.astype(BF16)
        add_bias_sums(gq, 6, h)
    grads[2 * D + width : 2 * D + 2 * width, :] = dot(gp_t[0:width, :], attn_in[...]).astype(BF16)
    ar_start(4)
    ar_steps("b1", "e0", "c1", "a2", "e1", "b2")

    def late_pass(slot):
        @pl.when(jnp.logical_not(early) & (slot < a))
        def _():
            pass_down(slot)

    late_pass(0)
    ar_steps("c2", "a3", "e2", "b3")
    late_pass(1)
    ar_steps("c3", "e3")

    @pl.when(b == 0)
    def _():
        dx_copy(a).wait_recv()

    @pl.when(a < m - 1)
    def _():
        dz_copy(a, below).wait_recv()

    for h in range(heads):
        top = h * HD
        own_sum = dkv[1, lax.rem(a, slots), h].astype(F32)
        own_sum += jnp.where(b == 0, dkx[a, h].astype(F32), 0.0)
        own_sum += jnp.where(a < m - 1, dkz[a, h].astype(F32), 0.0)
        own_t = jnp.transpose(own_sum)
        gk = rotate_rows(own_t[0:HD], cos, -sin)
        gv = own_t[HD:]
        gp_t[width + top : width + top + HD, :] = gk.astype(BF16)
        gp_t[2 * width + top : 2 * width + top + HD, :] = gv.astype(BF16)
        add_bias_sums(gv, 7, h)

    gp_all = gp_t[...]
    for i in range(2):
        grads[2 * D + (2 + i) * width : 2 * D + (3 + i) * width, :] = dot(
            gp_t[(1 + i) * width : (2 + i) * width, :], attn_in[...]
        ).astype(BF16)
        ar_start(5 + i)
    for i in range(rows // step):
        where = slice(i * step, (i + 1) * step)
        gat = dot(gp_all[:, where], wqkv_ref[...], TN)
        parts[2][i * step // own : (i + 1) * step // own] = gat.astype(BF16).reshape(-1, own, D)
        if i == 0:
            vec[0:1, :] = jnp.sum(gat * hat[where, :], axis=0, keepdims=True)
            vec[1:2, :] = jnp.sum(gat, axis=0, keepdims=True)
        else:
            vec[0:1, :] += jnp.sum(gat * hat[where, :], axis=0, keepdims=True)
            vec[1:2, :] += jnp.sum(gat, axis=0, keepdims=True)
    tp_a(2)

    vx = copy(vec, vec_x, vx_send, vx_recv, (xp, t))
    vx.start()
    tp_b(2)
    tp_c(0)
    ar_steps("a4", "b4", "f0")
    vx.wait_recv()
    vec_pair[...] = vec[...] + vec_x[...]

    def vz_copy(k):
        return copy(
            vec_pair, vec_z.at[k], vz_send.at[k], vz_recv.at[k], (2 * ((a + k + 1) % m) + b, t)
        )

    for k in range(m - 1):
        vz_copy(k).start()
    ar_steps("a5", "c4", "b5", "a6", "f1")
    total = vec_pair[...]
    for k in range(m - 1):
        vz_copy(k).wait_recv()
        total += vec_z[k]
    vec_ctx[...] = total

    def vt_copy(k, dev):
        return copy(vec_ctx, vec_tp.at[k], vt_send.at[k], vt_recv.at[k], dev)

    for k, dev in enumerate((sib, peer, diag)):
        vt_copy(k, (c, dev)).start()
    ar_steps("e4", "c5", "b6", "f2")

    tp_c(2)
    mine = pl.ds(pl.multiple_of(t * own, own), own)
    x = x_ref[...].astype(F32)
    mean = jnp.mean(x, axis=1, keepdims=True)
    cen = x - mean
    inv = lax.rsqrt(jnp.mean(cen * cen, axis=1, keepdims=True) + EPS)
    h1 = hat[mine, :]
    out_ref[...] = (x + parts_own[0] + as_row(denseb_ref) + as_row(downb_ref)).astype(BF16)

    def norm_back(dh, gain):
        gh = dh * gain
        return inv * (
            gh - jnp.mean(gh, axis=1, keepdims=True) - h1 * jnp.mean(gh * h1, axis=1, keepdims=True)
        )

    gin_ref[...] = (
        c_ref[...].astype(F32) + norm_back(parts_own[2], gain1) + norm_back(parts_own[1], gain2)
    )
    for k in range(3):
        vt_copy(k, (c, sib)).wait_recv()
    small_ref[0:5, :] = vec_ctx[0:5, :] + vec_tp[0, 0:5, :] + vec_tp[1, 0:5, :] + vec_tp[2, 0:5, :]
    small_ref[5:8, :] = vec_ctx[5:8, :]
    ar_steps("e5", "c6", "e6", "f3", "f4", "f5", "f6")
    for i in range(len(SEGMENTS)):
        ar_far(i)

    for i in range(2):
        src, dst = ((x_ref, xg), (c_ref, cg))[i]
        copy(src, dst.at[t], tg_send.at[i, 0], tg_recv.at[i, t], (c, peer)).wait_send()
        copy(src, dst.at[t], tg_send.at[i, 1], tg_recv.at[i, t], (c, sib)).wait_send()

    copy(cg.at[peer], cg.at[peer], tf_send.at[1], tg_recv.at[1, peer], (c, sib)).wait_send()

    @pl.when(a < m - 1)
    def _():
        def up_done(d, carry):
            j = 2 * d + b
            copy(kv.at[j], kv.at[j], kv_up_send.at[j], kv_recv.at[j], (xp, t)).wait_send()
            return carry

        lax.fori_loop(0, a + 1, up_done, 0)

    def x_done(d, carry):
        j = 2 * d + b
        copy(kv.at[j], kv.at[j], kv_x_send.at[j], kv_recv.at[j], (xp, t)).wait_send()
        return carry

    lax.fori_loop(0, a, x_done, 0)

    def down_done(d, carry):
        dx_copy(d).wait_send()
        dz_copy(d, below).wait_send()
        return carry

    lax.fori_loop(jnp.maximum(a - slots + 1, 0), a, down_done, 0)

    @pl.when(b == 0)
    def _():
        copy(kv.at[c], kv.at[c], kv_x_send.at[c], kv_recv.at[c], (xp, t)).wait_send()

    @pl.when(b == 1)
    def _():
        dx_copy(a).wait_send()

    for p in range(3):
        pc_copy(p, 0).wait_send()
        pc_copy(p, 1).wait_send()
        py_copy(p).wait_send()
    for i in range(len(SEGMENTS)):
        ar_end(i)
    vx.wait_send()
    for k in range(m - 1):
        vz_copy(k).wait_send()
    for k in range(3):
        vt_copy(k, (c, sib)).wait_send()


def layer(n, heads, own, *args):
    rows = args[2].shape[0]
    m = n // 2
    hidden = D
    vmem, dma = pltpu.VMEM, pltpu.SemaphoreType.DMA
    scratch = [
        vmem((rows // own, own, D), BF16),
        vmem((rows // own, own, D), BF16),
        vmem((rows, D), F32),
        vmem((rows, D), BF16),
        vmem((rows, D), BF16),
        vmem((n, heads, 2 * HD, rows), BF16),
        vmem((heads, HD, rows), BF16),
        vmem((heads, HD, rows), BF16),
        vmem((heads, rows, 2 * HD), BF16),
        vmem((heads, rows, 2 * HD), BF16),
        vmem((rows // own, own, hidden), BF16),
        vmem((rows // own, own, hidden), BF16),
        vmem((rows, D), F32),
        vmem((heads, 1, rows), F32),
        vmem((heads, 1, rows), F32),
        vmem((heads, HD, rows), F32),
        vmem((heads * HD, rows), BF16),
        vmem((heads, 1, rows), F32),
        vmem((2, 4 if m <= 4 else 2, heads, rows, 2 * HD), BF16),
        vmem((m, heads, rows, 2 * HD), BF16),
        vmem((m, heads, rows, 2 * HD), BF16),
        vmem((3 * heads * HD, rows), BF16),
        vmem((ROWS, D), BF16),
        vmem((ROWS, D), BF16),
        vmem((ROWS // 2, D), BF16),
        vmem((ROWS // 4, D), BF16),
        vmem((3, 2, own, D), BF16),
        vmem((3, own, D), BF16),
        vmem((3, own, D), BF16),
        vmem((3, own, D), F32),
        vmem((8, D), F32),
        vmem((8, D), F32),
        vmem((8, D), F32),
        vmem((m - 1, 8, D), F32),
        vmem((8, D), F32),
        vmem((3, 8, D), F32),
        dma((2, 2)),
        dma((2, 4)),
        dma((2,)),
        dma((n,)),
        dma((n,)),
        dma((n,)),
        dma((m,)),
        dma((m,)),
        dma((m,)),
        dma((m,)),
        *[dma((len(SEGMENTS),))] * 6,
        dma((len(SEGMENTS), 4, 3)),
        dma((len(SEGMENTS), 4)),
        dma((3, 2)),
        dma((3, 2)),
        dma((3,)),
        dma((3,)),
        dma(()),
        dma(()),
        dma((m - 1,)),
        dma((m - 1,)),
        dma((3,)),
        dma((3,)),
    ]
    return pl.pallas_call(
        functools.partial(layer_kernel, n, heads),
        out_shape=[
            jax.ShapeDtypeStruct((own, D), BF16),
            jax.ShapeDtypeStruct((own, D), F32),
            jax.ShapeDtypeStruct((ROWS, D), BF16),
            jax.ShapeDtypeStruct((8, D), F32),
        ],
        in_specs=[pl.BlockSpec(memory_space=pltpu.VMEM)] * len(args),
        out_specs=[pl.BlockSpec(memory_space=pltpu.VMEM)] * 4,
        scratch_shapes=scratch,
        compiler_params=pltpu.CompilerParams(
            collective_id=1, has_side_effects=True, vmem_limit_bytes=62 * 1024 * 1024
        ),
        name="layer",
    )(*args)


def local(
    inputs,
    positions,
    attn_scale,
    attn_shift,
    mlp_scale,
    mlp_shift,
    qkv_weight,
    qv_bias,
    dense_weight,
    dense_bias,
    up_weight,
    up_bias,
    down_weight,
    down_bias,
    cotangent,
):
    width = qkv_weight.shape[2]
    heads = width // HD
    n = lax.axis_size("ctx")
    wqkv = jnp.transpose(qkv_weight, (1, 2, 0)).reshape(3 * width, D)
    output, grad_input, fin, small = layer(
        n,
        heads,
        inputs.shape[0],
        inputs,
        cotangent,
        positions,
        attn_scale,
        attn_shift,
        mlp_scale,
        mlp_shift,
        dense_bias,
        down_bias,
        wqkv,
        qv_bias,
        dense_weight,
        up_weight,
        up_bias,
        down_weight,
    )
    grad_qkv = fin[2 * D + width :].astype(F32).reshape(3, width, D)
    return (
        output,
        grad_input,
        small[0],
        small[1],
        small[2],
        small[3],
        jnp.transpose(grad_qkv, (2, 0, 1)),
        small[6:8, :width],
        fin[2 * D : 2 * D + width].astype(F32),
        small[4],
        fin[D : 2 * D].astype(F32),
        small[5],
        fin[:D].astype(F32),
        small[4],
    )


def solution(mesh):
    in_specs = (
        P(("ctx", "tp"), None),
        P("ctx"),
        P(),
        P(),
        P(),
        P(),
        P(None, None, "tp"),
        P(None, "tp"),
        P("tp", None),
        P(),
        P(None, "tp"),
        P("tp"),
        P("tp", None),
        P(),
        P(("ctx", "tp"), None),
    )
    out_specs = (
        P(("ctx", "tp"), None),
        P(("ctx", "tp"), None),
        P(),
        P(),
        P(),
        P(),
        P(None, None, "tp"),
        P(None, "tp"),
        P("tp", None),
        P(),
        P(None, "tp"),
        P("tp"),
        P("tp", None),
        P(),
    )
    return jax.shard_map(local, mesh=mesh, in_specs=in_specs, out_specs=out_specs, check_vma=False)
```
